32 devices in a mesh: gx: 4 (over z), gy: 4 (over x, core), gz: 2 (over y).
Axes of the slice: x: 2, y: 2, z: 4, core: 2. Of those that a mesh axis runs over, the one named last changes fastest.
Arguments:
- dist: float32 [19, 8, 32, 512], P(None, 'gx', 'gy', 'gz'), may hold values from 0.01 to 0.1
- site_kinds: int32 [8, 32, 512], P('gx', 'gy', 'gz'), may hold values from 0 to 3
- relax: float32 [8, 32, 512], P('gx', 'gy', 'gz'), may hold values from 0.5 to 1.9
- inflow: float32 [3, 8, 32, 512], P(None, 'gx', 'gy', 'gz'), may hold values from -0.3 to 0.3
Outputs:
- density: float32 [8, 32, 512], P('gx', 'gy', 'gz')
- momentum: float32 [3, 8, 32, 512], P(None, 'gx', 'gy', 'gz')
The draws below stay inside these ranges and needn't reach their ends.
All inputs are finite; a program needn't handle non-finite values.
Results may differ from the reference program's by a relative error of at most 0.0001.
Values sent between devices are 32-bit elements; how exact they have to be, the bound alone decides.
No kernel may reach another device: no remote copies, remote signals or barrier semaphores. Data moves between devices by JAX's collectives and lax.ppermute only.
A program may use at most 64 MiB of HBM per device.

```python
import math
import jax
import jax.numpy as jnp
import numpy as np

STEPS = 2
NX = 8
NY = 32
NZ = 512


def with_ends(values, own_key, low, high):
    dims = values.shape
    place = [jax.random.randint(jax.random.fold_in(own_key, axis), (), 0, dims[axis]) for axis in range(len(dims))]
    values = values.at[tuple(place)].set(low)
    longest = dims.index(max(dims))
    place[longest] = (place[longest] + 1) % dims[longest]
    return values.at[tuple(place)].set(high)


def steps_of(rng, shape, split, smallest, top_value):
    level, own = 1.0, jax.random.fold_in(rng, 6)
    for position, blocks in split:
        draws = jnp.exp(jax.random.uniform(jax.random.fold_in(own, position), (blocks,), jnp.float32, smallest / len(split), top_value / len(split)))
        level = level * jnp.repeat(draws, shape[position] // blocks).reshape([-1 if axis == position else 1 for axis in range(len(shape))])
    return level


def setup_inputs(seed: int = 0) -> dict:
    arg_keys = jax.random.split(jax.random.key(seed), 5)
    return {
        "dist": jnp.clip(0.01 + 0.09 * jax.random.uniform(arg_keys[0], (19, NX, NY, NZ), jnp.float32) ** steps_of(arg_keys[0], (19, NX, NY, NZ), ((1, 4), (2, 4), (3, 2)), -0.2, 0.2), 0.01, 0.1),
        "site_kinds": with_ends(jax.random.randint(arg_keys[1], (NX, NY, NZ), 0, 4), jax.random.fold_in(arg_keys[1], 1), 0, 3).astype(jnp.int32),
        "relax": jnp.clip(jnp.exp(math.log(1.9) - 1.3350011 * jax.random.uniform(arg_keys[2], (NX, NY, NZ), jnp.float32) ** steps_of(arg_keys[2], (NX, NY, NZ), ((0, 4), (1, 4), (2, 2)), -0.2, 0.2)), 0.5, 1.9),
        "inflow": jnp.clip(jax.random.uniform(arg_keys[3], (3, NX, NY, NZ), jnp.float32, -0.3, 0.3) * steps_of(arg_keys[3], (3, NX, NY, NZ), ((1, 4), (2, 4), (3, 2)), -0.4, 0.0), -0.3, 0.3),
    }


VELOCITIES = [(0, 0, 0), (1, 0, 0), (-1, 0, 0), (0, 1, 0), (0, -1, 0), (0, 0, 1), (0, 0, -1),
              (1, 1, 0), (-1, -1, 0), (1, -1, 0), (-1, 1, 0), (1, 0, 1), (-1, 0, -1),
              (1, 0, -1), (-1, 0, 1), (0, 1, 1), (0, -1, -1), (0, 1, -1), (0, -1, 1)]
WEIGHTS = [1.0 / 3.0] + [1.0 / 18.0] * 6 + [1.0 / 36.0] * 12
OPPOSITE = [0, 2, 1, 4, 3, 6, 5, 8, 7, 10, 9, 12, 11, 14, 13, 16, 15, 18, 17]


def moments(dist):
    table = np.array(VELOCITIES, dtype=np.float32)
    density = jnp.sum(dist, axis=0)
    parts = []
    for axis_id in range(3):
        column = jnp.asarray(table[:, axis_id]).astype(dist.dtype)
        parts.append(jnp.sum(column[:, None, None, None] * dist, axis=0))
    return density, jnp.stack(parts)


def equilibrium(density, speed):
    usq = speed[0] * speed[0] + speed[1] * speed[1] + speed[2] * speed[2]
    result = []
    for index in range(19):
        vel = VELOCITIES[index]
        along = vel[0] * speed[0] + vel[1] * speed[1] + vel[2] * speed[2]
        result.append(WEIGHTS[index] * (density + 3.0 * along + 4.5 * along * along - 1.5 * usq))
    return jnp.stack(result)


def collide(dist, site_kinds, relax, inflow):
    density, speed = moments(dist)
    fluid = dist - relax[None] * (dist - equilibrium(density, speed))
    wall = dist[np.array(OPPOSITE)]
    inlet = equilibrium(density, inflow)
    outlet = equilibrium(jnp.ones_like(density), speed)
    kinds = site_kinds[None]
    return jnp.where(kinds == 0, wall, jnp.where(kinds == 1, fluid, jnp.where(kinds == 2, inlet, outlet)))


def reference(dist, site_kinds, relax, inflow):
    field = dist
    for step in range(STEPS):
        post = collide(field, site_kinds, relax, inflow)
        padded = jnp.pad(post, ((0, 0), (1, 1), (1, 1), (1, 1)))
        moved = []
        for index in range(19):
            vel = VELOCITIES[index]
            moved.append(padded[index, 1 - vel[0]:1 - vel[0] + NX, 1 - vel[1]:1 - vel[1] + NY, 1 - vel[2]:1 - vel[2] + NZ])
        field = jnp.stack(moved)
    return moments(field)
```

```python
import functools

import jax
import jax.numpy as jnp
import numpy as np
from jax import lax
from jax.experimental import pallas as pl
from jax.experimental.pallas import tpu as pltpu
from jax.sharding import PartitionSpec as P

AXES = ("gx", "gy", "gz")
VEL = [
    (0, 0, 0),
    (1, 0, 0), (-1, 0, 0), (0, 1, 0), (0, -1, 0), (0, 0, 1), (0, 0, -1),
    (1, 1, 0), (-1, -1, 0), (1, -1, 0), (-1, 1, 0),
    (1, 0, 1), (-1, 0, -1), (1, 0, -1), (-1, 0, 1),
    (0, 1, 1), (0, -1, -1), (0, 1, -1), (0, -1, 1),
]
IDX = {v: i for i, v in enumerate(VEL)}
NQ = len(VEL)
OPP = [IDX[tuple(-a for a in v)] for v in VEL]
PAIRS = [(i, OPP[i]) for i in range(1, NQ) if i < OPP[i]]
NA = 5
NV = NQ + NA


def mirror(i, axis):
    v = list(VEL[i])
    v[axis] = -v[axis]
    return IDX[tuple(v)]


UP = [[i for i in range(NQ) if VEL[i][a] == 1] for a in range(3)]
DN = [[mirror(i, a) for i in UP[a]] for a in range(3)]
LV = [[i for i in range(NQ) if VEL[i][a] == 0] for a in range(3)]
AUX = list(range(NQ, NV))


def weight(i):
    return {0: 1.0 / 3.0, 1: 1.0 / 18.0, 2: 1.0 / 36.0}[sum(abs(c) for c in VEL[i])]


def combine(coefs, parts):
    total = None
    for c, p in zip(coefs, parts):
        if c == 0:
            continue
        if total is None:
            total = p if c > 0 else -p
        else:
            total = total + p if c > 0 else total - p
    return total


def raw_moments(f):
    rho = f[0]
    mom = [None, None, None]
    for i, j in PAIRS:
        rho = rho + (f[i] + f[j])
        diff = f[i] - f[j]
        for a in range(3):
            c = VEL[i][a]
            if c:
                if mom[a] is None:
                    mom[a] = diff if c > 0 else -diff
                else:
                    mom[a] = mom[a] + diff if c > 0 else mom[a] - diff
    return rho, mom


class Site:
    def __init__(self, f, aux):
        code, relax, vin = aux[0], aux[1], aux[2:]
        rho, mom = raw_moments(f)
        fluid = code == 2.0
        inlet = code == 3.0
        self.wall = code == 1.0
        self.keep = jnp.where(fluid, 1.0 - relax, 0.0)
        gain = jnp.where(fluid, relax, jnp.where(code > 2.5, 1.0, 0.0))
        r = jnp.where(code == 4.0, 1.0, rho)
        self.u3 = [3.0 * jnp.where(inlet, v, m) for v, m in zip(vin, mom)]
        sq = self.u3[0] * self.u3[0] + self.u3[1] * self.u3[1] + self.u3[2] * self.u3[2]
        self.base = r - sq * (1.0 / 6.0)
        self.gain = {w: gain * w for w in (1.0 / 3.0, 1.0 / 18.0, 1.0 / 36.0)}

    def post(self, vel, wgt, f, f_opp):
        a = combine(vel, self.u3)
        s = self.base if a is None else self.base + (0.5 * a * a + a)
        return jnp.where(self.wall, f_opp, self.keep * f + self.gain[wgt] * s)

    def post_pair(self, vel, wgt, f, f_opp):
        a = combine(vel, self.u3)
        s = self.base + 0.5 * a * a
        g = self.gain[wgt]
        return (
            jnp.where(self.wall, f_opp, self.keep * f + g * (s + a)),
            jnp.where(self.wall, f, self.keep * f_opp + g * (s - a)),
        )

    def post_all(self, f):
        out = [None] * NQ
        out[0] = self.post(VEL[0], weight(0), f[0], f[0])
        for i, j in PAIRS:
            out[i], out[j] = self.post_pair(VEL[i], weight(i), f[i], f[j])
        return out


def odd_mask(axis, shape):
    return jnp.full(shape, lax.rem(lax.axis_index(axis), 2), jnp.int32) == 1


def side_masks(axis, size, shape):
    me = lax.axis_index(axis)
    index = jnp.full(shape, me, jnp.int32)
    return index > 0, index < size - 1


def halves(even, odd, axis, size, shape):
    is_odd = odd_mask(axis, shape)
    low, high = side_masks(axis, size, shape)

    def pick(e, o):
        if o is None:
            return (
                jnp.where(low & is_odd, e, 0.0),
                jnp.where(high & ~is_odd, e, 0.0),
            )
        return (
            jnp.where(low, jnp.where(is_odd, e, o), 0.0),
            jnp.where(high, jnp.where(is_odd, o, e), 0.0),
        )

    return pick


def iota(shape, axis):
    return lax.broadcasted_iota(jnp.int32, shape, axis)


def roll(x, shift, axis):
    shift = shift % x.shape[axis]
    return x if shift == 0 else pltpu.roll(x, shift, axis)


def first_kernel(two, dist, kinds, relax, inflow, post, code, xe, *xo):
    lx, ly, lz = dist.shape[1:]
    for x in range(lx):
        c = kinds[x].astype(jnp.float32) + 1.0
        code[x] = c
        f = [dist[i, x] for i in range(NQ)]
        aux = [c, relax[x]] + [inflow[a, x] for a in range(3)]
        for i, p in enumerate(Site(f, aux).post_all(f)):
            post[i, x] = p

    def value(v, x):
        if v < NQ:
            return post[v, x]
        return [code, relax][v - NQ][x] if v < NQ + 2 else inflow[v - NQ - 2, x]

    is_odd = odd_mask("gx", (ly, lz))
    up = [(i, lx - 2) for i in UP[0]] + [(i, lx - 1) for i in UP[0] + LV[0] + AUX]
    down = [(i, 1) for i in DN[0]] + [(i, 0) for i in DN[0] + LV[0] + AUX]
    for k, (u, d) in enumerate(zip(up, down)):
        to_up, to_down = value(*u), value(*d)
        xe[k] = jnp.where(is_odd, to_down, to_up)
        if two:
            xo[0][k] = jnp.where(is_odd, to_up, to_down)


def plane_value(post, code, relax, inflow, halo):
    lx = post.shape[1]
    n = len(UP[0])

    def value(v, x):
        if v >= NQ:
            if x < 0:
                return halo[0, n + len(UP[0]) + len(LV[0]) + v - NQ]
            if x >= lx:
                return halo[1, n + len(UP[0]) + len(LV[0]) + v - NQ]
            return [code, relax][v - NQ][x] if v < NQ + 2 else inflow[v - NQ - 2, x]
        c = VEL[v][0]
        if c == 0:
            if x < 0:
                return halo[0, 2 * n + LV[0].index(v)]
            if x >= lx:
                return halo[1, 2 * n + LV[0].index(v)]
            return post[v, x]
        if 0 <= x - c < lx:
            return post[v, x - c]
        if c > 0:
            return halo[0, (n if x == 0 else 0) + UP[0].index(v)]
        return halo[1, (n if x == lx - 1 else 0) + DN[0].index(v)]

    return value


Y_UP = [(i, 2) for i in UP[1]] + [(i, 1) for i in UP[1] + LV[1] + AUX]
Y_DN = [(i, 2) for i in DN[1]] + [(i, 1) for i in DN[1] + LV[1] + AUX]


def second_kernel(nx, two_x, two_y, post, code, relax, inflow, *refs):
    refs = list(refs)
    re = refs.pop(0)
    ro = refs.pop(0) if two_x else None
    halo, ye = refs.pop(0), refs.pop(0)
    yo = refs.pop(0) if two_y else None
    lx, ly, lz = post.shape[1:]
    shape = (ly, lz)
    pick = halves(re, ro, "gx", nx, shape)
    for k in range(re.shape[0]):
        low, high = pick(re[k], None if ro is None else ro[k])
        halo[0, k] = low
        halo[1, k] = high
    value = plane_value(post, code, relax, inflow, halo)
    row = iota(shape, 0)
    is_odd = odd_mask("gy", shape)
    planes = lx + 2
    per = ly // planes
    for t in range(NV // per):
        up = down = None
        for h in range(per):
            (u, du), (d, dd) = Y_UP[per * t + h], Y_DN[per * t + h]
            for x in range(planes):
                j = h * planes + x
                a = roll(value(u, x - 1), j - (ly - du), 0)
                b = roll(value(d, x - 1), j - (dd - 1), 0)
                up = a if up is None else jnp.where(row == j, a, up)
                down = b if down is None else jnp.where(row == j, b, down)
        ye[t] = jnp.where(is_odd, down, up)
        if two_y:
            yo[t] = jnp.where(is_odd, up, down)


def third_kernel(ny, two_y, two_z, post, code, relax, inflow, halo, *refs):
    refs = list(refs)
    ye = refs.pop(0)
    yo = refs.pop(0) if two_y else None
    re = refs.pop(0)
    ro = refs.pop(0) if two_y else None
    moved, ze = refs.pop(0), refs.pop(0)
    zo = refs.pop(0) if two_z else None
    lx, ly, lz = post.shape[1:]
    shape = (ly, lz)
    value = plane_value(post, code, relax, inflow, halo)
    row = iota(shape, 0)
    planes = lx + 2
    per = ly // planes
    is_odd = odd_mask("gy", shape)
    pick = halves(re, ro, "gy", ny, shape)
    tiles = NV // per
    got_low, got_high, own_up, own_down = [], [], [], []
    for t in range(tiles):
        low, high = pick(re[t], None if ro is None else ro[t])
        got_low.append(low)
        got_high.append(high)
        e = ye[t]
        o = e if yo is None else yo[t]
        own_up.append(jnp.where(is_odd, o, e))
        own_down.append(jnp.where(is_odd, e, o))
    if yo is None:
        for t in range(tiles):
            up = down = None
            for h in range(per):
                (u, du), (d, dd) = Y_UP[per * t + h], Y_DN[per * t + h]
                for x in range(planes):
                    j = h * planes + x
                    a = roll(value(u, x - 1), j - (ly - du), 0)
                    b = roll(value(d, x - 1), j - (dd - 1), 0)
                    up = a if up is None else jnp.where(row == j, a, up)
                    down = b if down is None else jnp.where(row == j, b, down)
            own_up[t], own_down[t] = up, down

    def group(tiles_of, slot, dst):
        return roll(tiles_of[slot // per], (dst - slot % per) * planes, 0)

    first = row < planes
    n = len(UP[1])
    for v in range(NV):
        c = VEL[v][1] if v < NQ else 0
        if c > 0:
            p = UP[1].index(v)
            edge = jnp.where(first, group(got_low, p, 0), group(own_up, n + p, 1))
        elif c < 0:
            p = DN[1].index(v)
            edge = jnp.where(first, group(own_down, n + p, 0), group(got_high, p, 1))
        else:
            p = 2 * n + (LV[1].index(v) if v < NQ else len(LV[1]) + v - NQ)
            edge = jnp.where(first, group(got_low, p, 0), group(got_high, p, 1))
        moved[v, planes] = edge
        for x in range(planes):
            q = value(v, x - 1)
            if c > 0:
                s = n + UP[1].index(v)
                line = roll(got_low[s // per], -((s % per) * planes + x), 0)
                q = jnp.where(row == 0, line, roll(q, 1, 0))
            elif c < 0:
                s = n + DN[1].index(v)
                line = roll(got_high[s // per], ly - 1 - ((s % per) * planes + x), 0)
                q = jnp.where(row == ly - 1, line, roll(q, -1, 0))
            moved[v, x] = q

    lanes = 128
    small = (ly, lanes)
    lane = iota(small, 1)
    up = jnp.zeros(small, jnp.float32)
    down = jnp.zeros(small, jnp.float32)
    n = len(UP[2])
    for t in range(planes + 1):
        for p, (u, d) in enumerate(zip(UP[2], DN[2])):
            at = NV * t + 2 * p
            here = (lane == at) | (lane == at + 1)
            up = jnp.where(here, roll(moved[u, t, :, lz - lanes :], at - (lanes - 2), 1), up)
            down = jnp.where(here, roll(moved[d, t, :, :lanes], at, 1), down)
        for q, v in enumerate(LV[2] + AUX):
            at = NV * t + 2 * n + q
            here = lane == at
            up = jnp.where(here, roll(moved[v, t, :, lz - lanes :], at - (lanes - 1), 1), up)
            down = jnp.where(here, roll(moved[v, t, :, :lanes], at, 1), down)
    is_odd = odd_mask("gz", small)
    ze[...] = jnp.where(is_odd, down, up)
    if two_z:
        zo[...] = jnp.where(is_odd, up, down)


def final_moments(moved, lx):
    planes = lx + 2
    post = {}
    for t in range(planes):
        f = [roll(moved(i, t), VEL[i][2], 1) for i in range(NQ)]
        site = Site(f, [moved(v, t) for v in AUX])
        if t == 0 or t == planes - 1:
            for i in UP[0] if t == 0 else DN[0]:
                post[i, t] = site.post(VEL[i], weight(i), f[i], f[OPP[i]])
        else:
            for i, p in enumerate(site.post_all(f)):
                post[i, t] = p
    t = planes
    f = [roll(moved(i, t), VEL[i][2], 1) for i in range(NQ)]
    site = Site(f, [moved(v, t) for v in AUX])
    shape = f[0].shape
    ly = shape[0]
    row = iota(shape, 0)
    first = row < planes
    site.u3[1] = jnp.where(first, site.u3[1], -site.u3[1])
    edge = {}
    for u, d in zip(UP[1], DN[1]):
        edge[VEL[u][0], VEL[u][2]] = site.post(
            VEL[u],
            weight(u),
            jnp.where(first, f[u], f[d]),
            jnp.where(first, f[OPP[u]], f[OPP[d]]),
        )

    def shifted(main, cy, lines):
        at, base = (0, 0) if cy > 0 else (ly - 1, planes)
        line = combine([s for s, _, _ in lines], [roll(e, at - (base + p), 0) for _, e, p in lines])
        return jnp.where(row == at, line, roll(main, cy, 0))

    result = []
    for t in range(1, lx + 1):

        def get(cx, cy, cz):
            return post[IDX[cx, cy, cz], t - cx]

        density = get(0, 0, 0) + get(1, 0, 0) + get(-1, 0, 0)
        mx = get(1, 0, 0) - get(-1, 0, 0)
        my = None
        for cy in (1, -1):
            centre, plus, minus = get(0, cy, 0), get(1, cy, 0), get(-1, cy, 0)
            ec, ep, em = edge[0, 0], edge[1, 0], edge[-1, 0]
            total = shifted(centre + (plus + minus), cy, [(1, ec, t), (1, ep, t - 1), (1, em, t + 1)])
            mx = mx + shifted(plus - minus, cy, [(1, ep, t - 1), (-1, em, t + 1)])
            density = density + total
            my = total if my is None else my - total
        mz = None
        for cz in (1, -1):
            plus, minus = get(1, 0, cz), get(-1, 0, cz)
            a = shifted(get(0, 1, cz), 1, [(1, edge[0, cz], t)])
            b = shifted(get(0, -1, cz), -1, [(1, edge[0, cz], t)])
            total = roll(get(0, 0, cz) + (plus + minus) + (a + b), cz, 1)
            mx = mx + roll(plus - minus, cz, 1)
            my = my + roll(a - b, cz, 1)
            density = density + total
            mz = total if mz is None else mz - total
        result.append([density, mx, my, mz])
    return result


def last_kernel(nz, two_z, moved, *refs):
    refs = list(refs)
    re = refs.pop(0)
    ro = refs.pop(0) if two_z else None
    density, momentum = refs
    planes = moved.shape[1] - 1
    lx = planes - 2
    ly, lz = moved.shape[2:]
    lanes = 128
    small = (ly, lanes)
    lane = iota(small, 1)
    low, high = halves(re, ro, "gz", nz, small)(re[...], None if ro is None else ro[...])
    n = len(UP[2])
    half, most = lanes // 2, lanes - lanes // 4

    def seam(v, t):
        x = jnp.where(lane < most, roll(moved[v, t, :, :lanes], half, 1), moved[v, t, :, lz - lanes :])
        c = VEL[v][2] if v < NQ else 0
        if c > 0:
            at = NV * t + 2 * UP[2].index(v)
            return jnp.where((lane == half - 1) | (lane == half - 2), roll(low, half - 2 - at, 1), x)
        if c < 0:
            at = NV * t + 2 * DN[2].index(v)
            return jnp.where(lane < 2, roll(high, -at, 1), x)
        at = NV * t + 2 * n + (LV[2].index(v) if v < NQ else len(LV[2]) + v - NQ)
        x = jnp.where(lane == half - 1, roll(low, half - 1 - at, 1), x)
        return jnp.where(lane == 0, roll(high, -at, 1), x)

    inner = final_moments(lambda v, t: moved[v, t], lx)
    rim = final_moments(seam, lx)
    for x in range(lx):
        for a in range(4):
            main, edge = inner[x][a], rim[x][a]
            parts = [main[:, k * lanes : (k + 1) * lanes] for k in range(lz // lanes)]
            parts[0] = jnp.where(lane < 2, roll(edge, -half, 1), parts[0])
            parts[-1] = jnp.where(lane >= lanes - 2, edge, parts[-1])
            for k, p in enumerate(parts):
                if a == 0:
                    density[x, :, k * lanes : (k + 1) * lanes] = p
                else:
                    momentum[a - 1, x, :, k * lanes : (k + 1) * lanes] = p


def pair_routes(sizes):
    def linear(c):
        return (c[0] * sizes[1] + c[1]) * sizes[2] + c[2]

    routes = []
    for axis in range(3):
        own = []
        for odd in range(2 if sizes[axis] > 2 else 1):
            spare = [a for a in (1, 2, 0) if a != axis and sizes[a] % 2 == 0]
            route = []
            for c in np.ndindex(*sizes):
                other = list(c)
                k = ((c[axis] - odd) ^ 1) + odd
                if 0 <= k < sizes[axis]:
                    other[axis] = k
                elif spare:
                    other[spare[0]] ^= 1
                else:
                    continue
                route.append((linear(c), linear(other)))
            own.append(route)
        routes.append(own)
    return routes


def swap(messages, routes):
    return [lax.ppermute(m, AXES, r) for m, r in zip(messages, routes)]


def call(body, outs, flops, *args):
    size = sum(int(np.prod(a.shape)) * 4 for a in args) + sum(int(np.prod(s)) * 4 for s in outs)
    return pl.pallas_call(
        body,
        out_shape=[jax.ShapeDtypeStruct(s, jnp.float32) for s in outs],
        in_specs=[pl.BlockSpec(memory_space=pltpu.VMEM)] * len(args),
        out_specs=[pl.BlockSpec(memory_space=pltpu.VMEM)] * len(outs),
        cost_estimate=pl.CostEstimate(flops=flops, bytes_accessed=size, transcendentals=0),
    )(*args)


def shards(sizes, dist, site_kinds, relax, inflow):
    lx, ly, lz = dist.shape[1:]
    routes = pair_routes(sizes)
    two = [len(r) == 2 for r in routes]
    planes = lx + 2
    block = lx * ly * lz
    xs, ys = (NV, ly, lz), (NV * planes // ly, ly, lz)
    post, code, *xm = call(
        functools.partial(first_kernel, two[0]),
        [dist.shape, site_kinds.shape] + [xs] * len(routes[0]),
        250 * block,
        dist, site_kinds, relax, inflow,
    )
    xr = swap(xm, routes[0])
    halo, *ym = call(
        functools.partial(second_kernel, sizes[0], two[0], two[1]),
        [(2,) + xs] + [ys] * len(routes[1]),
        100 * block,
        post, code, relax, inflow, *xr,
    )
    yr = swap(ym, routes[1])
    moved, *zm = call(
        functools.partial(third_kernel, sizes[1], two[1], two[2]),
        [(NV, planes + 1, ly, lz)] + [(ly, 128)] * len(routes[2]),
        100 * block,
        post, code, relax, inflow, halo, *ym, *yr,
    )
    zr = swap(zm, routes[2])
    density, momentum = call(
        functools.partial(last_kernel, sizes[2], two[2]),
        [(lx, ly, lz), (3, lx, ly, lz)],
        400 * block,
        moved, *zr,
    )
    return density, momentum


def solution(mesh):
    sizes = tuple(mesh.shape[a] for a in AXES)
    return jax.shard_map(
        functools.partial(shards, sizes),
        mesh=mesh,
        in_specs=(
            P(None, "gx", "gy", "gz"),
            P("gx", "gy", "gz"),
            P("gx", "gy", "gz"),
            P(None, "gx", "gy", "gz"),
        ),
        out_specs=(P("gx", "gy", "gz"), P(None, "gx", "gy", "gz")),
        check_vma=False,
    )
```

```python
import functools

import jax
import jax.numpy as jnp
import numpy as np
from jax import lax
from jax.experimental import pallas as pl
from jax.experimental.pallas import tpu as pltpu
from jax.sharding import PartitionSpec as P


AXES = ("gx", "gy", "gz")
VEL = [
    (0, 0, 0),
    (1, 0, 0), (-1, 0, 0), (0, 1, 0), (0, -1, 0), (0, 0, 1), (0, 0, -1),
    (1, 1, 0), (-1, -1, 0), (1, -1, 0), (-1, 1, 0),
    (1, 0, 1), (-1, 0, -1), (1, 0, -1), (-1, 0, 1),
    (0, 1, 1), (0, -1, -1), (0, 1, -1), (0, -1, 1),
]
IDX = {v: i for i, v in enumerate(VEL)}
NQ = len(VEL)
OPP = [IDX[tuple(-a for a in v)] for v in VEL]
PAIRS = [(i, OPP[i]) for i in range(1, NQ) if i < OPP[i]]
NA = 5
NV = NQ + NA
LANES = 128


def mirror(i, axis):
    v = list(VEL[i])
    v[axis] = -v[axis]
    return IDX[tuple(v)]


UP = [[i for i in range(NQ) if VEL[i][a] == 1] for a in range(3)]
DN = [[mirror(i, a) for i in UP[a]] for a in range(3)]
LV = [[i for i in range(NQ) if VEL[i][a] == 0] for a in range(3)]
AUX = list(range(NQ, NV))


def weight(i):
    return {0: 1.0 / 3.0, 1: 1.0 / 18.0, 2: 1.0 / 36.0}[sum(abs(c) for c in VEL[i])]


def combine(coefs, parts):
    total = None
    for c, p in zip(coefs, parts):
        if c == 0:
            continue
        if total is None:
            total = p if c > 0 else -p
        else:
            total = total + p if c > 0 else total - p
    return total


def raw_moments(f):
    rho = f[0]
    mom = [None, None, None]
    for i, j in PAIRS:
        rho = rho + (f[i] + f[j])
        diff = f[i] - f[j]
        for a in range(3):
            c = VEL[i][a]
            if c:
                if mom[a] is None:
                    mom[a] = diff if c > 0 else -diff
                else:
                    mom[a] = mom[a] + diff if c > 0 else mom[a] - diff
    return rho, mom


class Site:
    def __init__(self, f, aux):
        code, relax, vin = aux[0], aux[1], aux[2:]
        rho, mom = raw_moments(f)
        fluid = code == 2.0
        inlet = code == 3.0
        self.wall = code == 1.0
        self.keep = jnp.where(fluid, 1.0 - relax, 0.0)
        gain = jnp.where(fluid, relax, jnp.where(code > 2.5, 1.0, 0.0))
        r = jnp.where(code == 4.0, 1.0, rho)
        self.u3 = [3.0 * jnp.where(inlet, v, m) for v, m in zip(vin, mom)]
        sq = self.u3[0] * self.u3[0] + self.u3[1] * self.u3[1] + self.u3[2] * self.u3[2]
        self.base = r - sq * (1.0 / 6.0)
        self.gain = {w: gain * w for w in (1.0 / 3.0, 1.0 / 18.0, 1.0 / 36.0)}

    def post(self, vel, wgt, f, f_opp):
        a = combine(vel, self.u3)
        s = self.base if a is None else self.base + (0.5 * a * a + a)
        return jnp.where(self.wall, f_opp, self.keep * f + self.gain[wgt] * s)

    def post_pair(self, vel, wgt, f, f_opp):
        a = combine(vel, self.u3)
        s = self.base + 0.5 * a * a
        g = self.gain[wgt]
        return (
            jnp.where(self.wall, f_opp, self.keep * f + g * (s + a)),
            jnp.where(self.wall, f, self.keep * f_opp + g * (s - a)),
        )

    def post_all(self, f):
        out = [None] * NQ
        out[0] = self.post(VEL[0], weight(0), f[0], f[0])
        for i, j in PAIRS:
            out[i], out[j] = self.post_pair(VEL[i], weight(i), f[i], f[j])
        return out


    def edge_rows(self, f, first):
        self.u3[1] = jnp.where(first, self.u3[1], -self.u3[1])
        edge = {}
        for u, d in zip(UP[1], DN[1]):
            edge[VEL[u][0], VEL[u][2]] = self.post(
                VEL[u],
                weight(u),
                jnp.where(first, f[u], f[d]),
                jnp.where(first, f[OPP[u]], f[OPP[d]]),
            )
        return edge


def odd_mask(axis, shape):
    return jnp.full(shape, lax.rem(lax.axis_index(axis), 2), jnp.int32) == 1


def side_masks(axis, size, shape):
    me = lax.axis_index(axis)
    index = jnp.full(shape, me, jnp.int32)
    return index > 0, index < size - 1


def halves(axis, size, shape):
    is_odd = odd_mask(axis, shape)
    low, high = side_masks(axis, size, shape)

    def pick(e, o):
        if o is None:
            return (
                jnp.where(low & is_odd, e, 0.0),
                jnp.where(high & ~is_odd, e, 0.0),
            )
        return (
            jnp.where(low, jnp.where(is_odd, e, o), 0.0),
            jnp.where(high, jnp.where(is_odd, o, e), 0.0),
        )

    return pick


def iota(shape, axis):
    return lax.broadcasted_iota(jnp.int32, shape, axis)


def roll(x, shift, axis):
    shift = shift % x.shape[axis]
    return x if shift == 0 else pltpu.roll(x, shift, axis)


Y_UP = [(i, 2) for i in UP[1]] + [(i, 1) for i in UP[1] + LV[1] + AUX]
Y_DN = [(i, 2) for i in DN[1]] + [(i, 1) for i in DN[1] + LV[1] + AUX]


def source(v, x, lx):
    c = VEL[v][0] if v < NQ else 0
    x -= c
    if x < 0:
        return 0, x + lx
    if x >= lx:
        return 1, x - lx
    return None, x


def edge_rows(side, lx):
    return [
        (way, k, x)
        for way, slots in enumerate((Y_UP, Y_DN))
        for k, (v, _) in enumerate(slots)
        for x in range(-1, lx + 1)
        if source(v, x, lx)[0] == side
    ]


def row_of(way, k, ly):
    return ly - Y_UP[k][1] if way == 0 else Y_DN[k][1] - 1


def pop_of(way, k):
    return (Y_UP, Y_DN)[way][k][0]


def bulk_planes(side, lx):
    near, far = (-1, 0) if side == 0 else (lx, lx - 1)
    away = (UP, DN)[side][0]
    return [(i, near) for i in away] + [(i, far) for i in away] + [(i, near) for i in LV[0] + AUX]


def gather_rows(rows, ly):
    tiles = []
    for base in range(0, len(rows), ly):
        total = None
        for j, (tile, r) in enumerate(rows[base : base + ly]):
            part = roll(tile, j - r, 0)
            total = part if total is None else jnp.where(iota(part.shape, 0) == j, part, total)
        tiles.append(total)
    return tiles


def first_kernel(two, dist, kinds, relax, inflow, post, aux, *refs):
    refs = list(refs)
    edge = [refs.pop(0) for _ in range(1 + two)]
    bulk = [refs.pop(0) for _ in range(1 + two)]
    dist_v, kinds_v, sems = refs
    copies = [
        pltpu.make_async_copy(kinds, kinds_v, sems.at[0]),
        pltpu.make_async_copy(relax, aux.at[1], sems.at[1]),
        pltpu.make_async_copy(inflow, aux.at[pl.ds(2, 3)], sems.at[2]),
        pltpu.make_async_copy(dist, dist_v, sems.at[3]),
    ]
    for c in copies:
        c.start()
    for c in copies:
        c.wait()
    lx, ly, lz = dist.shape[1:]
    for x in range(lx):
        aux[0, x] = kinds_v[x].astype(jnp.float32) + 1.0
        f = [dist_v[i, x] for i in range(NQ)]
        for i, p in enumerate(Site(f, [aux[a, x] for a in range(NA)]).post_all(f)):
            post[i, x] = p

    def sent(v, x):
        plane = source(v, x, lx)[1]
        return post[v, plane] if v < NQ else aux[v - NQ, plane]

    is_odd = odd_mask("gx", (ly, lz))

    def put(refs, k, to_up, to_down):
        refs[0][k] = jnp.where(is_odd, to_down, to_up)
        if two:
            refs[1][k] = jnp.where(is_odd, to_up, to_down)

    sides = [
        gather_rows([(sent(pop_of(w, k), x), row_of(w, k, ly)) for w, k, x in edge_rows(s, lx)], ly)
        for s in (0, 1)
    ]
    for k, (u, d) in enumerate(zip(*sides)):
        put(edge, k, u, d)
    for k, (u, d) in enumerate(zip(bulk_planes(0, lx), bulk_planes(1, lx))):
        put(bulk, k, sent(*u), sent(*d))


def second_kernel(nx, two_x, post, aux, *refs):
    refs = list(refs)
    re = refs.pop(0)
    ro = refs.pop(0) if two_x else None
    ys = refs
    lx, ly, lz = post.shape[1:]
    pick = halves("gx", nx, (ly, lz))
    got = [pick(re[k], None if ro is None else ro[k]) for k in range(re.shape[0])]
    where = {}
    for side in (0, 1):
        for n, item in enumerate(edge_rows(side, lx)):
            where[item] = (got[n // ly][side], n % ly)
    tiles = []
    for way in (0, 1):
        rows = []
        for k in range(NV):
            v = pop_of(way, k)
            for x in range(-1, lx + 1):
                side, plane = source(v, x, lx)
                if side is not None:
                    rows.append(where[way, k, x])
                else:
                    rows.append((post[v, plane] if v < NQ else aux[v - NQ, plane], row_of(way, k, ly)))
        tiles.append(gather_rows(rows, ly))
    is_odd = odd_mask("gy", (ly, lz))
    for t, (up, down) in enumerate(zip(*tiles)):
        ys[0][t] = jnp.where(is_odd, down, up)
        ys[1][t] = jnp.where(is_odd, up, down)


def third_kernel(nx, ny, two_x, two_y, two_z, post, aux, *refs):
    refs = list(refs)
    xe = refs.pop(0)
    xo = refs.pop(0) if two_x else None
    ys = [refs.pop(0), refs.pop(0)]
    re = refs.pop(0)
    ro = refs.pop(0) if two_y else None
    moved, ze = refs.pop(0), refs.pop(0)
    zo = refs.pop(0) if two_z else None
    lx, ly, lz = post.shape[1:]
    shape = (ly, lz)
    row = iota(shape, 0)
    planes = lx + 2
    per = ly // planes
    pick = halves("gx", nx, shape)
    halo = {}
    for k, (u, d) in enumerate(zip(bulk_planes(0, lx), bulk_planes(1, lx))):
        halo[u], halo[d] = pick(xe[k], None if xo is None else xo[k])

    def value(v, x):
        side, plane = source(v, x, lx)
        if side is not None:
            return halo[v, x]
        return post[v, plane] if v < NQ else aux[v - NQ, plane]

    is_odd = odd_mask("gy", shape)
    pick = halves("gy", ny, shape)
    got_low, got_high, own_up, own_down = [], [], [], []
    for t in range(NV // per):
        low, high = pick(re[t], None if ro is None else ro[t])
        got_low.append(low)
        got_high.append(high)
        e, o = ys[0][t], ys[1][t]
        own_up.append(jnp.where(is_odd, o, e))
        own_down.append(jnp.where(is_odd, e, o))

    def group(tiles, slot, dst):
        return roll(tiles[slot // per], (dst - slot % per) * planes, 0)

    first = row < planes
    n = len(UP[1])
    for v in range(NV):
        c = VEL[v][1] if v < NQ else 0
        if c > 0:
            p = UP[1].index(v)
            edge = jnp.where(first, group(got_low, p, 0), group(own_up, n + p, 1))
        elif c < 0:
            p = DN[1].index(v)
            edge = jnp.where(first, group(own_down, n + p, 0), group(got_high, p, 1))
        else:
            p = 2 * n + (LV[1].index(v) if v < NQ else len(LV[1]) + v - NQ)
            edge = jnp.where(first, group(got_low, p, 0), group(got_high, p, 1))
        moved[v, planes] = edge
        for x in range(planes):
            q = value(v, x - 1)
            if c > 0:
                s = n + UP[1].index(v)
                line = roll(got_low[s // per], -((s % per) * planes + x), 0)
                q = jnp.where(row == 0, line, roll(q, 1, 0))
            elif c < 0:
                s = n + DN[1].index(v)
                line = roll(got_high[s // per], ly - 1 - ((s % per) * planes + x), 0)
                q = jnp.where(row == ly - 1, line, roll(q, -1, 0))
            moved[v, x] = q

    small = (ly, LANES)
    lane = iota(small, 1)
    up = jnp.zeros(small, jnp.float32)
    down = jnp.zeros(small, jnp.float32)
    for t in range(planes + 1):
        for p, (u, d) in enumerate(zip(UP[2], DN[2])):
            at = NV * t + 2 * p
            here = (lane == at) | (lane == at + 1)
            up = jnp.where(here, roll(moved[u, t, :, lz - LANES :], at + 2, 1), up)
            down = jnp.where(here, roll(moved[d, t, :, :LANES], at, 1), down)
        for q, v in enumerate(LV[2] + AUX):
            at = NV * t + 2 * len(UP[2]) + q
            here = lane == at
            up = jnp.where(here, roll(moved[v, t, :, lz - LANES :], at + 1, 1), up)
            down = jnp.where(here, roll(moved[v, t, :, :LANES], at, 1), down)
    is_odd = odd_mask("gz", small)
    ze[...] = jnp.where(is_odd, down, up)
    if two_z:
        zo[...] = jnp.where(is_odd, up, down)


def last_move(get, shifted, line):
    plus, minus = get(1, 0, 0), get(-1, 0, 0)
    density = get(0, 0, 0) + (plus + minus)
    mx = plus - minus
    lp, lm = line[1, 0], line[-1, 0]
    line_sum, line_diff = line[0, 0] + (lp + lm), lp - lm
    ways = []
    for cy in (1, -1):
        plus, minus = get(1, cy, 0), get(-1, cy, 0)
        ways.append(shifted(get(0, cy, 0) + (plus + minus), cy, line_sum))
        mx = mx + shifted(plus - minus, cy, line_diff)
    density = density + (ways[0] + ways[1])
    my = ways[0] - ways[1]
    ways = []
    for cz in (1, -1):
        plus, minus = get(1, 0, cz), get(-1, 0, cz)
        a = shifted(get(0, 1, cz), 1, line[0, cz])
        b = shifted(get(0, -1, cz), -1, line[0, cz])
        ways.append(roll(get(0, 0, cz) + (plus + minus) + (a + b), cz, 1))
        mx = mx + roll(plus - minus, cz, 1)
        my = my + roll(a - b, cz, 1)
    return density + (ways[0] + ways[1]), mx, my, ways[0] - ways[1]


def final_moments(moved, lx):
    planes = lx + 2
    post = {}
    for t in range(planes + 1):
        f = [roll(moved(i, t), VEL[i][2], 1) for i in range(NQ)]
        site = Site(f, [moved(v, t) for v in AUX])
        if t == planes:
            row = iota(f[0].shape, 0)
            edge = site.edge_rows(f, row < planes)
        elif t == 0 or t == planes - 1:
            for i in UP[0] if t == 0 else DN[0]:
                post[i, t] = site.post(VEL[i], weight(i), f[i], f[OPP[i]])
        else:
            for i, p in enumerate(site.post_all(f)):
                post[i, t] = p
    ly = row.shape[0]
    line = {k: (e if k[0] == 0 else roll(e, k[0], 0)) for k, e in edge.items()}
    result = []
    for t in range(1, lx + 1):

        def get(cx, cy, cz):
            return post[IDX[cx, cy, cz], t - cx]

        def shifted(main, cy, line):
            at, base = (0, 0) if cy > 0 else (ly - 1, planes)
            return jnp.where(row == at, roll(line, at - (base + t), 0), roll(main, cy, 0))

        result.append(last_move(get, shifted, line))
    return result


CUT = 4
HIGH, LOW, START = CUT, CUT + 2, CUT + 4


def inner_kernel(moved, inner, seam):
    planes = moved.shape[1] - 1
    ly, lz = moved.shape[2:]
    lane = iota((ly, LANES), 1)
    for v in range(NV):
        total = jnp.zeros((ly, LANES), jnp.float32)
        for t in range(planes + 1):
            at = NV * t
            last = roll(moved[v, t, :, lz - LANES :], at + CUT, 1)
            start = roll(moved[v, t, :, :LANES], at + START, 1)
            total = jnp.where((lane >= at) & (lane < at + CUT), last, total)
            total = jnp.where((lane >= at + START) & (lane < at + START + CUT), start, total)
        seam[v] = total
    for x, parts in enumerate(final_moments(lambda v, t: moved[v, t], planes - 2)):
        for a, p in enumerate(parts):
            inner[a, x] = p


def rim_kernel(nz, two_z, inner, seam, *refs):
    refs = list(refs)
    re = refs.pop(0)
    ro = refs.pop(0) if two_z else None
    density, momentum = refs
    lx, ly, lz = density.shape
    planes = lx + 2
    small = (ly, LANES)
    lane, row = iota(small, 1), iota(small, 0)
    low, high = halves("gz", nz, small)(re[...], None if ro is None else ro[...])

    def lanes_of(*places):
        mask = None
        for t in range(planes + 1):
            for p in places:
                here = lane == NV * t + p
                mask = here if mask is None else mask | here
        return mask

    two_low, two_high = lanes_of(LOW, LOW + 1), lanes_of(HIGH, HIGH + 1)
    one_low, one_high = lanes_of(LOW + 1), lanes_of(HIGH)

    def value(v):
        x = seam[v]
        c = VEL[v][2] if v < NQ else 0
        if c > 0:
            return jnp.where(two_low, roll(low, LOW - 2 * UP[2].index(v), 1), x)
        if c < 0:
            return jnp.where(two_high, roll(high, HIGH - 2 * DN[2].index(v), 1), x)
        at = 2 * len(UP[2]) + (LV[2].index(v) if v < NQ else len(LV[2]) + v - NQ)
        x = jnp.where(one_low, roll(low, LOW + 1 - at, 1), x)
        return jnp.where(one_high, roll(high, HIGH - at, 1), x)

    f = [roll(value(i), VEL[i][2], 1) for i in range(NQ)]
    site = Site(f, [value(v) for v in AUX])
    post = site.post_all(f)
    first = row < planes
    edge = site.edge_rows(f, first)
    near = {k: (e if k[0] == 0 else roll(e, k[0], 0)) for k, e in edge.items()}

    def get(cx, cy, cz):
        return roll(post[IDX[cx, cy, cz]], NV * cx, 1)

    def shifted(main, cy, line):
        at, base = (0, 0) if cy > 0 else (ly - 1, planes)
        out = roll(main, cy, 0)
        for t in range(1, lx + 1):
            part = roll(roll(line, NV * (t - planes), 1), at - (base + t), 0)
            out = jnp.where((row == at) & (lane >= NV * t) & (lane < NV * (t + 1)), part, out)
        return out

    total = last_move(get, shifted, near)
    for x in range(lx):
        for a in range(4):
            at = NV * (x + 1)
            parts = [inner[a, x, :, k : k + LANES] for k in range(0, lz, LANES)]
            parts[0] = jnp.where(lane < 2, roll(total[a], -(at + START), 1), parts[0])
            parts[-1] = jnp.where(lane >= LANES - 2, roll(total[a], -(at + CUT), 1), parts[-1])
            for k, p in enumerate(parts):
                if a == 0:
                    density[x, :, k * LANES : (k + 1) * LANES] = p
                else:
                    momentum[a - 1, x, :, k * LANES : (k + 1) * LANES] = p


def pair_routes(sizes):
    def linear(c):
        return (c[0] * sizes[1] + c[1]) * sizes[2] + c[2]

    routes = []
    for axis in range(3):
        own = []
        for odd in range(2 if sizes[axis] > 2 else 1):
            spare = [a for a in (1, 2, 0) if a != axis and sizes[a] % 2 == 0]
            route = []
            for c in np.ndindex(*sizes):
                other = list(c)
                k = ((c[axis] - odd) ^ 1) + odd
                if 0 <= k < sizes[axis]:
                    other[axis] = k
                elif spare:
                    other[spare[0]] ^= 1
                else:
                    continue
                route.append((linear(c), linear(other)))
            own.append(route)
        routes.append(own)
    return routes


def swap(messages, routes):
    return [lax.ppermute(m, AXES, r) for m, r in zip(messages, routes)]


VMEM = pl.BlockSpec(memory_space=pltpu.VMEM)
HBM = pl.BlockSpec(memory_space=pltpu.HBM)


def call(body, outs, flops, *args, specs=None, scratch=()):
    size = sum(int(np.prod(a.shape)) * 4 for a in args) + sum(int(np.prod(s)) * 4 for s in outs)
    return pl.pallas_call(
        body,
        out_shape=[jax.ShapeDtypeStruct(s, jnp.float32) for s in outs],
        in_specs=specs or [VMEM] * len(args),
        out_specs=[VMEM] * len(outs),
        scratch_shapes=scratch,
        cost_estimate=pl.CostEstimate(flops=flops, bytes_accessed=size, transcendentals=0),
        compiler_params=pltpu.CompilerParams(vmem_limit_bytes=16 << 20),
    )(*args)


def shards(sizes, dist, site_kinds, relax, inflow):
    lx, ly, lz = dist.shape[1:]
    planes = lx + 2
    assert ly == 2 * planes and lz % LANES == 0 and lz > LANES
    routes = pair_routes(sizes)
    two = [len(r) == 2 for r in routes]
    block = lx * ly * lz
    bulk, edge, ys = (NV, ly, lz), (-(-len(edge_rows(0, lx)) // ly), ly, lz), (NV * planes // ly, ly, lz)
    post, aux, *xm = call(
        functools.partial(first_kernel, two[0]),
        [dist.shape, (NA,) + site_kinds.shape] + [edge] * len(routes[0]) + [bulk] * len(routes[0]),
        250 * block,
        *[pltpu.with_memory_space_constraint(a, pltpu.HBM) for a in (dist, site_kinds, relax, inflow)],
        specs=[HBM] * 4,
        scratch=[
            pltpu.VMEM(dist.shape, jnp.float32),
            pltpu.VMEM(site_kinds.shape, jnp.int32),
            pltpu.SemaphoreType.DMA((4,)),
        ],
    )
    n = len(routes[0])
    xr = swap(xm[:n], routes[0])
    br = swap(xm[n:], routes[0])
    ym = call(
        functools.partial(second_kernel, sizes[0], two[0]),
        [ys, ys],
        100 * block,
        post, aux, *xr,
    )
    yr = swap(ym, routes[1])
    moved, *zm = call(
        functools.partial(third_kernel, sizes[0], sizes[1], two[0], two[1], two[2]),
        [(NV, planes + 1, ly, lz)] + [(ly, LANES)] * len(routes[2]),
        100 * block,
        post, aux, *br, *ym, *yr,
    )
    zr = swap(zm, routes[2])
    inner, seam = call(inner_kernel, [(4, lx, ly, lz), (NV, ly, LANES)], 300 * block, moved)
    density, momentum = call(
        functools.partial(rim_kernel, sizes[2], two[2]),
        [(lx, ly, lz), (3, lx, ly, lz)],
        100 * block,
        inner, seam, *zr,
    )
    return density, momentum


def solution(mesh):
    sizes = tuple(mesh.shape[a] for a in AXES)

    def body(*args):
        return shards(sizes, *args)

    return jax.shard_map(
        body,
        mesh=mesh,
        in_specs=(
            P(None, "gx", "gy", "gz"),
            P("gx", "gy", "gz"),
            P("gx", "gy", "gz"),
            P(None, "gx", "gy", "gz"),
        ),
        out_specs=(P("gx", "gy", "gz"), P(None, "gx", "gy", "gz")),
        check_vma=False,
    )
```
